32 devices in a mesh: member: 4 (over y, core), patch: 8 (over z, x).
Axes of the slice: x: 2, y: 2, z: 4, core: 2. Of those that a mesh axis runs over, the one named last changes fastest.
Arguments:
- kernel_rows: bfloat16 [2048, 2048], P('patch'), as said below
- row_scale: float32 [2048], P('patch'), may hold values from 0.3 to 1
- self_stiffness: float32 [2048], P('patch'), may hold values from 1 to 3
- base_stress: float32 [2048], P('patch'), may hold values from 0.5 to 2.5
- friction_rate: float32 [2048], P('patch'), may hold values from 0.5 to 2
- damping: float32 [2048], P('patch'), may hold values from 0.5 to 2
- deficit_start: float32 [24, 2048], P('member', 'patch'), may hold values from -3 to 3
- state_start: float32 [24, 2048], P('member', 'patch'), may hold values from -1 to 1
- obs_rate: float32 [2048], P('patch'), may hold values from -6 to 6
- obs_precision: float32 [2048], P('patch'), may hold values from 0.2 to 2
Outputs:
- analysis: float32 [3, 24, 8, 256], P(None, None, 'patch', 'member')
The draws below stay inside these ranges and needn't reach their ends.
Inputs may be any that keep to these rules, and one draw needn't show every extreme that they name: `kernel_rows`: entries are independent with mean zero and root mean square of order 2048 ** -0.5 times a per-row factor.
All inputs are finite; a program needn't handle non-finite values.
Results may differ from the reference program's by a relative error of at most 0.0006.
Values may be sent and summed in bfloat16 or wider, within the bound.
A program may use at most 64 MiB of HBM per device.

```python
import math
import jax
import jax.numpy as jnp
from jax import lax

PATCH_DEV = 256
STEPS = 2
NEWTON = 4
NS_ITERS = 6
MARGIN = 8
PATCHES = 2048
ENSEMBLE = 24
BLOCK = 64
N_PATCH = 8


def draw_kernel_rows(key, part):
    entry_key = jax.random.fold_in(key, 11)
    spread = PATCHES ** (-0.5)
    values = jax.random.normal(entry_key, (PATCHES, PATCHES), jnp.float32) * spread
    return values.astype(jnp.bfloat16)


def block_scale(key, shape, pieces, least, top_value):
    def one(position, parts):
        steps = jax.random.uniform(jax.random.fold_in(jax.random.fold_in(key, 6), position), (parts,), jnp.float32, least / len(pieces), top_value / len(pieces))
        return jnp.repeat(jnp.exp(steps), shape[position] // parts).reshape((-1,) + (1,) * (len(shape) - position - 1))

    loudness = one(*pieces[0])
    for cut in pieces[1:]:
        loudness = loudness * one(*cut)
    return loudness


def gaussian(own_key, extent, width, limit, shards=(), kind=jnp.bfloat16):
    loudness = block_scale(own_key, extent, shards, -0.22, 0.18) if shards else 1.0
    array = jax.random.normal(own_key, extent, jnp.float32) * width * loudness
    return jnp.minimum(jnp.maximum(array, -limit), limit).astype(kind)


def setup_inputs(seed: int = 0) -> dict:
    key_of = jax.random.split(jax.random.key(seed), 11)
    return {
        "kernel_rows": draw_kernel_rows(jax.random.fold_in(key_of[10], 71), 0),
        "row_scale": jnp.clip(jnp.exp(math.log(1.0) - 1.2039728 * jax.random.uniform(key_of[1], (PATCHES,), jnp.float32) ** block_scale(key_of[1], (PATCHES,), ((0, 8),), -0.2, 0.2)), 0.3, 1.0),
        "self_stiffness": jnp.clip(jnp.exp(math.log(3.0) - 1.0986123 * jax.random.uniform(key_of[2], (PATCHES,), jnp.float32) ** block_scale(key_of[2], (PATCHES,), ((0, 8),), -0.2, 0.2)), 1.0, 3.0),
        "base_stress": jnp.clip(0.5 + 2.0 * jax.random.uniform(key_of[3], (PATCHES,), jnp.float32) ** block_scale(key_of[3], (PATCHES,), ((0, 8),), -0.2, 0.2), 0.5, 2.5),
        "friction_rate": jnp.clip(jnp.exp(math.log(2.0) - 1.3862944 * jax.random.uniform(key_of[4], (PATCHES,), jnp.float32) ** block_scale(key_of[4], (PATCHES,), ((0, 8),), -0.2, 0.2)), 0.5, 2.0),
        "damping": jnp.clip(jnp.exp(math.log(2.0) - 1.3862944 * jax.random.uniform(key_of[5], (PATCHES,), jnp.float32) ** block_scale(key_of[5], (PATCHES,), ((0, 8),), -0.2, 0.2)), 0.5, 2.0),
        "deficit_start": gaussian(key_of[6], (ENSEMBLE, PATCHES), 0.5, 3.0, ((0, 4), (1, 8)), jnp.float32),
        "state_start": jnp.clip(jax.random.uniform(key_of[7], (ENSEMBLE, PATCHES), jnp.float32, -1.0, 1.0) * block_scale(key_of[7], (ENSEMBLE, PATCHES), ((0, 4), (1, 8)), -0.4, 0.0), -1.0, 1.0),
        "obs_rate": gaussian(key_of[8], (PATCHES,), 1.0, 6.0, ((0, 8),), jnp.float32),
        "obs_precision": jnp.clip(jnp.exp(math.log(2.0) - 2.3025851 * jax.random.uniform(key_of[9], (PATCHES,), jnp.float32) ** block_scale(key_of[9], (PATCHES,), ((0, 8),), -0.2, 0.2)), 0.2, 2.0),
    }


time_step = 0.25
plate_rate = 1.0

def inverse_sinh(value):
    magnitude = jnp.abs(value)
    result = jnp.log(magnitude + jnp.sqrt(magnitude * magnitude + 1.0))
    return jnp.where(value < 0, -result, result)

def slip_rate(stress, state_log, guess, friction_rate, damping):
    factor = 0.5 * jnp.exp(state_log / friction_rate)
    velocity = guess
    for _ in range(NEWTON):
        scaled = factor * velocity
        residual = friction_rate * inverse_sinh(scaled) + damping * velocity - stress
        derivative = friction_rate * factor / jnp.sqrt(1.0 + scaled * scaled) + damping
        velocity = velocity - residual / derivative
    return velocity

def analyse(local_state, rate_window, obs_window):
    ensemble = rate_window.shape[0]
    window_width = rate_window.shape[1]
    sub_block = local_state.shape[2]
    margin = (window_width - sub_block) // 2
    highest = lax.Precision.HIGHEST
    mean_rate = lax.optimization_barrier(jnp.mean(rate_window, axis=0))
    anomalies = rate_window - mean_rate[None, :]
    innovation = obs_window[0] - mean_rate
    distance = jnp.abs(jnp.arange(sub_block, dtype=jnp.int32)[:, None] + margin - jnp.arange(window_width, dtype=jnp.int32)[None, :]).astype(jnp.float32)
    tapering = jnp.where(distance <= margin, jnp.exp(-0.5 * (distance / margin) ** 2), 0.0)
    weights = tapering * obs_window[1][None, :]
    weighted = anomalies[None, :, :] * weights[:, None, :]
    cross_terms = jnp.einsum('imj,nj->imn', weighted, anomalies, precision=highest)
    drive_terms = jnp.einsum('imj,j->im', weighted, innovation, precision=highest)
    identity = jnp.eye(ensemble, dtype=jnp.float32)
    scaling = ensemble - 1.0 + jnp.trace(cross_terms, axis1=1, axis2=2)
    root_part = ((ensemble - 1.0) * identity[None] + cross_terms) / scaling[:, None, None]
    inverse_root = jnp.broadcast_to(identity, root_part.shape)
    for _ in range(NS_ITERS):
        mixing = 1.5 * identity[None] - 0.5 * jnp.matmul(inverse_root, root_part, precision=highest)
        root_part = jnp.matmul(root_part, mixing, precision=highest)
        inverse_root = jnp.matmul(mixing, inverse_root, precision=highest)
    half_step = jnp.einsum('imn,in->im', inverse_root, drive_terms, precision=highest)
    mean_weight = jnp.einsum('imn,in->im', inverse_root, half_step, precision=highest) / scaling[:, None]
    spread = jnp.sqrt(ensemble - 1.0) * inverse_root / jnp.sqrt(scaling)[:, None, None]
    combined = spread + mean_weight[:, :, None]
    state_mean = lax.optimization_barrier(jnp.mean(local_state, axis=1))
    state_spread = local_state - state_mean[:, None, :]
    return state_mean[:, None, :] + jnp.einsum('vmi,imk->vki', state_spread, combined, precision=highest)

def reference(kernel_rows, row_scale, self_stiffness, base_stress, friction_rate, damping, deficit_start, state_start, obs_rate, obs_precision):
    kernel_wide = kernel_rows.astype(jnp.float32)

    def stress_of(deficit):
        rounded = lax.optimization_barrier(deficit.astype(jnp.bfloat16))
        coupled = jnp.dot(rounded.astype(jnp.float32), kernel_wide.T, precision=lax.Precision.HIGHEST)
        return base_stress + self_stiffness * deficit + row_scale * coupled

    def tendency(deficit, state_log, guess):
        velocity = slip_rate(stress_of(deficit), state_log, guess, friction_rate, damping)
        return (plate_rate - velocity, jnp.exp(-state_log) - jnp.abs(velocity), velocity)
    deficit = deficit_start
    state_log = state_start
    velocity = jnp.zeros_like(deficit_start)
    for _ in range(STEPS):
        deficit_zero, state_zero = (deficit, state_log)
        change, state_change, velocity = tendency(deficit_zero, state_zero, velocity)
        deficit_one = deficit_zero + time_step * change
        state_one = state_zero + time_step * state_change
        change, state_change, velocity = tendency(deficit_one, state_one, velocity)
        deficit_two = 0.75 * deficit_zero + 0.25 * (deficit_one + time_step * change)
        state_two = 0.75 * state_zero + 0.25 * (state_one + time_step * state_change)
        change, state_change, velocity = tendency(deficit_two, state_two, velocity)
        deficit = deficit_zero / 3.0 + 2.0 / 3.0 * (deficit_two + time_step * change)
        state_log = state_zero / 3.0 + 2.0 / 3.0 * (state_two + time_step * state_change)
    velocity = slip_rate(stress_of(deficit), state_log, velocity, friction_rate, damping)
    stacked = jnp.stack([deficit, state_log, velocity])
    ensemble = deficit.shape[0]
    blocks_total = PATCHES // BLOCK
    window_width = BLOCK + 2 * MARGIN
    positions = jnp.arange(blocks_total, dtype=jnp.int32)[:, None] * BLOCK + jnp.arange(window_width, dtype=jnp.int32)[None, :]
    padded_rate = jnp.pad(velocity, ((0, 0), (MARGIN, MARGIN)))
    padded_obs = jnp.pad(jnp.stack([obs_rate, obs_precision]), ((0, 0), (MARGIN, MARGIN)))
    rate_windows = jnp.transpose(padded_rate[:, positions], (1, 0, 2))
    obs_windows = jnp.transpose(padded_obs[:, positions], (1, 0, 2))
    state_blocks = jnp.transpose(stacked.reshape(3, ensemble, blocks_total, BLOCK), (2, 0, 1, 3))
    results = lax.map(lambda items: analyse(items[0], items[1], items[2]), (state_blocks, rate_windows, obs_windows))
    return jnp.transpose(results, (1, 2, 0, 3)).reshape(3, ensemble, N_PATCH, PATCH_DEV)
```

```python
import functools
import math

import jax
import jax.numpy as jnp
from jax import lax
from jax.experimental import pallas as pl
from jax.experimental.pallas import tpu as pltpu
from jax.sharding import PartitionSpec as P

STEPS = 2
NEWTON = 4
NS_ITERS = 6
MARGIN = 8
LANES = 128
TILE = 8

time_step = 0.25
plate_rate = 1.0

MESH = pl.DeviceIdType.MESH


def slip_rate(stress, state_log, guess, friction, inverse_friction, damping):
    factor = 0.5 * jnp.exp(state_log * inverse_friction)
    slope = friction * factor
    velocity = guess
    for _ in range(NEWTON):
        scaled = factor * velocity
        square = 1.0 + scaled * scaled
        inverse = lax.rsqrt(square)
        grown = jnp.log(jnp.abs(scaled) + square * inverse)
        grown = jnp.where(scaled < 0, -grown, grown)
        residual = friction * grown + damping * velocity - stress
        velocity = velocity - residual / (slope * inverse + damping)
    return velocity


def forecast_kernel(
    groups,
    count,
    kernel_hbm,
    row_scale_ref,
    stiffness_ref,
    base_ref,
    friction_ref,
    damping_ref,
    deficit_ref,
    state_ref,
    obs_rate_ref,
    obs_precision_ref,
    fields_out,
    kernel_ref,
    start_ref,
    gathered,
    packed,
    landed,
    lower,
    upper,
    load_sem,
    gather_send,
    gather_recv,
    move_send,
    move_recv,
    rim_send,
    rim_recv,
):
    member = lax.axis_index("member")
    patch = lax.axis_index("patch")
    members, own = deficit_ref.shape
    rows = start_ref.shape[1]
    sub_block = own // groups
    last = groups - 1

    load = pltpu.make_async_copy(kernel_hbm, kernel_ref, load_sem)
    load.start()

    lower[...] = jnp.zeros_like(lower)
    upper[...] = jnp.zeros_like(upper)
    start_ref[...] = jnp.zeros_like(start_ref)
    start_ref[0, 0:members] = deficit_ref[...]
    start_ref[1, 0:members] = state_ref[...]

    barrier = pltpu.get_barrier_semaphore()

    def greet(where):
        pl.semaphore_signal(barrier, inc=1, device_id=where, device_id_type=MESH)

    for shift in range(1, count):
        greet((member, lax.rem(patch + shift, count)))
    for shift in range(1, groups):
        greet((lax.rem(member + shift, groups), patch))

    after = lax.rem(patch + 1, count)
    before = lax.rem(patch + count - 1, count)
    greet((0, after))
    greet((last, before))

    @pl.when(member == 0)
    def _():
        for other in range(groups):
            greet((other, before))

    @pl.when(member == last)
    def _():
        for other in range(groups):
            greet((other, after))

    at_end = 1 - lax.div(member + last, groups) + lax.div(member + 1, groups)
    pl.semaphore_wait(barrier, count + groups + groups * at_end)

    row_scale = row_scale_ref[...]
    stiffness = stiffness_ref[...]
    base = base_ref[...]
    friction = friction_ref[...]
    damping = damping_ref[...]
    inverse_friction = 1.0 / friction

    stage = [0]

    def stress_of(deficit):
        slot = stage[0] % 2
        mine = gathered.at[slot, patch]
        gathered[slot, patch] = deficit.astype(jnp.bfloat16)
        copies = []
        for shift in range(1, count):
            copy = pltpu.make_async_remote_copy(
                src_ref=mine,
                dst_ref=mine,
                send_sem=gather_send.at[slot, shift],
                recv_sem=gather_recv.at[slot, shift],
                device_id=(member, lax.rem(patch + shift, count)),
                device_id_type=MESH,
            )
            copy.start()
            copies.append(copy)
        if stage[0] == 0:
            load.wait()
        for shift in range(1, count):
            source = gathered.at[slot, lax.rem(patch + count - shift, count)]
            pltpu.make_async_remote_copy(
                src_ref=source,
                dst_ref=source,
                send_sem=gather_send.at[slot, shift],
                recv_sem=gather_recv.at[slot, shift],
                device_id=(member, lax.rem(patch + count - shift, count)),
                device_id_type=MESH,
            ).wait_recv()
        summed = lax.dot_general(
            jnp.concatenate([gathered[slot, q] for q in range(count)], axis=1),
            kernel_ref[...],
            (((1,), (1,)), ((), ())),
            preferred_element_type=jnp.float32,
        )
        for copy in copies:
            copy.wait_send()
        stage[0] += 1
        return base + stiffness * deficit + row_scale * summed

    def rate(deficit, state_log, guess):
        return slip_rate(
            stress_of(deficit), state_log, guess, friction, inverse_friction, damping
        )

    def tendency(deficit, state_log, guess):
        velocity = rate(deficit, state_log, guess)
        return (plate_rate - velocity, jnp.exp(-state_log) - jnp.abs(velocity), velocity)

    deficit = start_ref[0]
    state_log = start_ref[1]
    velocity = jnp.zeros_like(deficit)
    for _ in range(STEPS):
        deficit_zero, state_zero = (deficit, state_log)
        change, state_change, velocity = tendency(deficit_zero, state_zero, velocity)
        deficit_one = deficit_zero + time_step * change
        state_one = state_zero + time_step * state_change
        change, state_change, velocity = tendency(deficit_one, state_one, velocity)
        deficit_two = 0.75 * deficit_zero + 0.25 * (deficit_one + time_step * change)
        state_two = 0.75 * state_zero + 0.25 * (state_one + time_step * state_change)
        change, state_change, velocity = tendency(deficit_two, state_two, velocity)
        deficit = deficit_zero / 3.0 + 2.0 / 3.0 * (deficit_two + time_step * change)
        state_log = state_zero / 3.0 + 2.0 / 3.0 * (state_two + time_step * state_change)
    velocity = rate(deficit, state_log, velocity)

    row = lax.broadcasted_iota(jnp.int32, (rows, own), 0)
    joined = jnp.where(row == members, obs_rate_ref[...], velocity)
    joined = jnp.where(row == members + 1, obs_precision_ref[...], joined)

    def window(cells, first):
        return pltpu.roll(cells, (-first) % own, 1)[:, :LANES]

    for group in range(groups):
        packed[group, 0:rows] = window(joined, group * sub_block - MARGIN)
        packed[group, rows : 2 * rows] = window(deficit, group * sub_block)
        packed[group, 2 * rows :] = window(state_log, group * sub_block)

    def move(shift):
        other = lax.rem(member + shift, groups)
        return pltpu.make_async_remote_copy(
            src_ref=packed.at[other],
            dst_ref=landed.at[shift],
            send_sem=move_send.at[shift],
            recv_sem=move_recv.at[shift],
            device_id=(other, patch),
            device_id_type=MESH,
        )

    def right_rim():
        return pltpu.make_async_remote_copy(
            src_ref=packed.at[0, 0:rows],
            dst_ref=lower.at[member],
            send_sem=rim_send.at[0],
            recv_sem=rim_recv.at[0, member],
            device_id=(0, after),
            device_id_type=MESH,
        )

    def left_rim():
        return pltpu.make_async_remote_copy(
            src_ref=packed.at[last, 0:rows],
            dst_ref=upper.at[member],
            send_sem=rim_send.at[1],
            recv_sem=rim_recv.at[1, member],
            device_id=(last, before),
            device_id_type=MESH,
        )

    right_rim().start()
    left_rim().start()

    for shift in range(1, groups):
        move(shift).start()

    landed[0] = packed[member]

    @pl.when(member == 0)
    def _():
        for other in range(groups):
            pltpu.make_async_remote_copy(
                src_ref=packed.at[0, 0:rows],
                dst_ref=lower.at[other],
                send_sem=rim_send.at[0],
                recv_sem=rim_recv.at[0, other],
                device_id=(other, before),
                device_id_type=MESH,
            ).wait_recv()

    @pl.when(member == last)
    def _():
        for other in range(groups):
            pltpu.make_async_remote_copy(
                src_ref=packed.at[0, 0:rows],
                dst_ref=upper.at[other],
                send_sem=rim_send.at[1],
                recv_sem=rim_recv.at[1, other],
                device_id=(other, after),
                device_id_type=MESH,
            ).wait_recv()

    for shift in range(1, groups):
        move(shift).wait_recv()

    lane = lax.broadcasted_iota(jnp.int32, (rows, LANES), 1)
    below = jnp.logical_and(lane < MARGIN, member == 0)
    above = jnp.logical_and(lane >= MARGIN + sub_block, member == last)
    start = jnp.logical_and(below, patch == 0)
    end = jnp.logical_and(above, patch == count - 1)
    outside = jnp.logical_or(start, jnp.logical_or(end, lane >= sub_block + 2 * MARGIN))
    for other in range(groups):
        held = landed[lax.rem(member - other + groups, groups)]
        cells = jnp.where(below, lower[other], held[0:rows])
        cells = jnp.where(above, upper[other], cells)
        cells = jnp.where(outside, 0.0, cells)
        fields_out[other, 0] = cells
        fields_out[other, 1] = held[rows : 2 * rows]
        fields_out[other, 2] = held[2 * rows :]

    for shift in range(1, groups):
        move(shift).wait_send()

    right_rim().wait_send()
    left_rim().wait_send()


def analysis_kernel(members, sub_block, fields_ref, out_ref, cross, mixing, kept, halfway):
    groups = fields_ref.shape[0]
    ensemble = groups * members
    split = LANES // sub_block
    per = ensemble // split
    extra = kept.shape[0] - per
    step = 24

    lane_row = lax.broadcasted_iota(jnp.int32, (1, LANES), 1)
    part = lane_row // sub_block

    def stacked(which):
        return jnp.concatenate(
            [fields_ref[g, which, 0:members] for g in range(groups)], axis=0
        )

    rates = stacked(0)
    observed = fields_ref[0, 0, members : members + 2]
    mean_rate = jnp.sum(rates, axis=0, keepdims=True) / ensemble
    anomalies = rates - mean_rate
    innovation = observed[0:1] - mean_rate
    weighted = anomalies * observed[1:2]

    source = lax.broadcasted_iota(jnp.int32, (LANES, LANES), 0)
    target = lax.broadcasted_iota(jnp.int32, (LANES, LANES), 1) % sub_block
    distance = jnp.abs(target + MARGIN - source).astype(jnp.float32)
    tapering = jnp.where(distance <= MARGIN, jnp.exp(-0.5 * (distance / MARGIN) ** 2), 0.0)

    def smooth(cells):
        return lax.dot_general(
            cells,
            tapering,
            (((1,), (0,)), ((), ())),
            precision=lax.Precision.HIGHEST,
            preferred_element_type=jnp.float32,
        )

    drive = smooth(weighted * innovation)
    trace = jnp.zeros((1, LANES), jnp.float32)
    for first in range(0, ensemble, step):
        products = jnp.concatenate(
            [weighted * anomalies[m : m + 1] for m in range(first, first + step)], axis=0
        )
        smoothed = smooth(products).reshape(step, ensemble, LANES)
        cross[first : first + step] = smoothed
        for m in range(step):
            trace = trace + smoothed[m, first + m : first + m + 1]
    scaling = ensemble - 1.0 + trace
    inverse_scaling = 1.0 / scaling

    column = lax.broadcasted_iota(jnp.int32, (ensemble, LANES), 0)

    def unit(m):
        return jnp.where(column == m, 1.0, 0.0)

    for m in range(ensemble):
        root = ((ensemble - 1.0) * unit(m) + cross[m]) * inverse_scaling
        mixing[m] = 1.5 * unit(m) - 0.5 * root
        cross[m] = root
    for r in range(per):
        root = cross[r]
        for g in range(1, split):
            root = jnp.where(part == g, cross[g * per + r], root)
        kept[r] = root

    fields = [stacked(1), stacked(2), pltpu.roll(rates, LANES - MARGIN, 1)]
    means = [jnp.sum(field, axis=0, keepdims=True) / ensemble for field in fields]
    vectors = [field - mean for field, mean in zip(fields, means)]
    for e in range(extra):
        filled = jnp.zeros((ensemble, LANES), jnp.float32)
        for t in range(e * split, min(e * split + split, 4)):
            g = t % split
            if t == 3:
                cells = drive
            else:
                cells = vectors[t]
                if g:
                    cells = pltpu.roll(cells, g * sub_block, 1)
            filled = jnp.where(part == g, cells, filled)
        kept[per + e] = filled

    def product(left, lo, hi, store):
        for first in range(0, ensemble, step):

            def some(base, sums):
                for k in range(TILE):
                    row = mixing[base + k, first : first + step]
                    sums = [
                        total + left[lo + i, pl.ds(base + k, 1)] * row
                        for i, total in enumerate(sums)
                    ]
                return sums

            sums = [jnp.zeros((step, LANES), jnp.float32) for _ in range(hi - lo)]
            if ensemble <= step:
                for base in range(0, ensemble, TILE):
                    sums = some(base, sums)
            else:
                sums = lax.fori_loop(
                    0, ensemble // TILE, lambda b, s: some(b * TILE, s), sums
                )
            for i, total in enumerate(sums):
                store(lo + i, first, total)

    def into(target):
        def store(i, first, total):
            target[i, first : first + step] = total

        return store

    def remix():
        for r in range(per):
            cells = kept[r]
            if split == 2:
                other = pltpu.roll(cells, sub_block, 1)
                spread = [jnp.where(part == 0, cells, other), jnp.where(part == 0, other, cells)]
            else:
                spread = []
                for g in range(split):
                    one = jnp.where(part == g, cells, 0.0)
                    width = sub_block
                    while width < LANES:
                        one = one + pltpu.roll(one, width, 1)
                        width *= 2
                    spread.append(one)
            for g in range(split):
                m = g * per + r
                mixing[m] = 1.5 * unit(m) - 0.5 * spread[g]

    def iterate(_, carry):
        product(kept, 0, per + extra, into(halfway))
        for e in range(extra):
            kept[per + e] = halfway[per + e]
        product(halfway, 0, per, into(kept))
        remix()
        return carry

    lax.fori_loop(0, NS_ITERS - 1, iterate, 0)
    product(kept, per, per + extra, into(halfway))

    def taken(t):
        cells = halfway[per + t // split]
        g = t % split
        return pltpu.roll(cells, LANES - g * sub_block, 1) if g else cells

    driven = taken(3)
    widening = math.sqrt(ensemble - 1.0) * lax.rsqrt(scaling)
    for v in range(3):
        spread = taken(v)
        moved = jnp.sum(spread * driven, axis=0, keepdims=True) * inverse_scaling
        result = means[v] + moved + widening * spread
        out_ref[v] = result[:, :sub_block]


def body(
    groups,
    count,
    kernel_rows,
    row_scale,
    self_stiffness,
    base_stress,
    friction_rate,
    damping,
    deficit_start,
    state_start,
    obs_rate,
    obs_precision,
):
    own, patches = kernel_rows.shape
    members = deficit_start.shape[0]
    ensemble = members * groups
    sub_block = own // groups
    rows = -(-(members + 2) // TILE) * TILE
    vmem = pl.BlockSpec(memory_space=pltpu.VMEM)
    f32 = jnp.float32

    fields = pl.pallas_call(
        functools.partial(forecast_kernel, groups, count),
        out_shape=jax.ShapeDtypeStruct((groups, 3, rows, LANES), f32),
        in_specs=[pl.BlockSpec(memory_space=pl.ANY)] + [vmem] * 9,
        out_specs=vmem,
        scratch_shapes=[
            pltpu.VMEM((own, patches), jnp.bfloat16),
            pltpu.VMEM((2, rows, own), f32),
            pltpu.VMEM((2, count, rows, own), jnp.bfloat16),
            pltpu.VMEM((groups, 3 * rows, LANES), f32),
            pltpu.VMEM((groups, 3 * rows, LANES), f32),
            pltpu.VMEM((groups, rows, LANES), f32),
            pltpu.VMEM((groups, rows, LANES), f32),
            pltpu.SemaphoreType.DMA,
            pltpu.SemaphoreType.DMA((2, count)),
            pltpu.SemaphoreType.DMA((2, count)),
            pltpu.SemaphoreType.DMA((groups,)),
            pltpu.SemaphoreType.DMA((groups,)),
            pltpu.SemaphoreType.DMA((2,)),
            pltpu.SemaphoreType.DMA((2, groups)),
        ],
        compiler_params=pltpu.CompilerParams(collective_id=0, has_side_effects=True),
    )(
        kernel_rows,
        *(
            cells.reshape(1, own)
            for cells in (row_scale, self_stiffness, base_stress, friction_rate, damping)
        ),
        deficit_start,
        state_start,
        obs_rate.reshape(1, own),
        obs_precision.reshape(1, own),
    )

    split = LANES // sub_block
    per = ensemble // split
    extra = -(-4 // split)
    analysis = pl.pallas_call(
        functools.partial(analysis_kernel, members, sub_block),
        out_shape=jax.ShapeDtypeStruct((3, ensemble, sub_block), f32),
        in_specs=[vmem],
        out_specs=vmem,
        scratch_shapes=[
            pltpu.VMEM((ensemble, ensemble, LANES), f32),
            pltpu.VMEM((ensemble, ensemble, LANES), f32),
            pltpu.VMEM((per + extra, ensemble, LANES), f32),
            pltpu.VMEM((per + extra, ensemble, LANES), f32),
        ],
    )(fields)
    return analysis[:, :, None, :]


def solution(mesh):
    return jax.shard_map(
        functools.partial(body, mesh.shape["member"], mesh.shape["patch"]),
        mesh=mesh,
        in_specs=(
            P("patch", None),
            P("patch"),
            P("patch"),
            P("patch"),
            P("patch"),
            P("patch"),
            P("member", "patch"),
            P("member", "patch"),
            P("patch"),
            P("patch"),
        ),
        out_specs=P(None, None, "patch", "member"),
        check_vma=False,
    )
```

```python
import functools
import math

import jax
import jax.numpy as jnp
from jax import lax
from jax.experimental import pallas as pl
from jax.experimental.pallas import tpu as pltpu
from jax.sharding import PartitionSpec as P

STEPS = 2
NEWTON = 4
NS_ITERS = 6
MARGIN = 8
LANES = 128
TILE = 8

time_step = 0.25
plate_rate = 1.0

MESH = pl.DeviceIdType.MESH


def slip_rate(stress, state_log, guess, friction, inverse_friction, damping):
    factor = 0.5 * jnp.exp(state_log * inverse_friction)
    slope = friction * factor
    velocity = guess
    for _ in range(NEWTON):
        scaled = factor * velocity
        square = 1.0 + scaled * scaled
        inverse = lax.rsqrt(square)
        grown = jnp.log(jnp.abs(scaled) + square * inverse)
        grown = jnp.where(scaled < 0, -grown, grown)
        residual = friction * grown + damping * velocity - stress
        velocity = velocity - residual / (slope * inverse + damping)
    return velocity


def forecast_kernel(
    groups,
    count,
    kernel_hbm,
    row_scale_ref,
    stiffness_ref,
    base_ref,
    friction_ref,
    damping_ref,
    deficit_ref,
    state_ref,
    obs_rate_ref,
    obs_precision_ref,
    fields_out,
    kernel_ref,
    start_ref,
    gathered,
    packed,
    landed,
    lower,
    upper,
    load_sem,
    gather_send,
    gather_recv,
    move_send,
    move_recv,
    rim_send,
    rim_recv,
):
    member = lax.axis_index("member")
    patch = lax.axis_index("patch")
    members, own = deficit_ref.shape
    rows = start_ref.shape[1]
    sub_block = own // groups
    last = groups - 1

    load = pltpu.make_async_copy(kernel_hbm, kernel_ref, load_sem)
    load.start()

    gathered[...] = jnp.zeros_like(gathered)
    lower[...] = jnp.zeros_like(lower)
    upper[...] = jnp.zeros_like(upper)
    start_ref[...] = jnp.zeros_like(start_ref)
    start_ref[0, 0:members] = deficit_ref[...]
    start_ref[1, 0:members] = state_ref[...]

    barrier = pltpu.get_barrier_semaphore()

    def greet(where):
        pl.semaphore_signal(barrier, inc=1, device_id=where, device_id_type=MESH)

    for shift in range(1, count):
        greet((member, lax.rem(patch + shift, count)))
    for shift in range(1, groups):
        greet((lax.rem(member + shift, groups), patch))

    after = lax.rem(patch + 1, count)
    before = lax.rem(patch + count - 1, count)
    has_after = 1 - lax.div(patch + 1, count)
    has_before = lax.div(patch + count - 1, count)
    takes_lower = (1 - lax.div(member + last, groups)) * has_before
    takes_upper = lax.div(member + 1, groups) * has_after

    @pl.when(has_after > 0)
    def _():
        greet((0, after))

    @pl.when(has_before > 0)
    def _():
        greet((last, before))

    @pl.when(takes_lower > 0)
    def _():
        for other in range(groups):
            greet((other, before))

    @pl.when(takes_upper > 0)
    def _():
        for other in range(groups):
            greet((other, after))

    rims = has_after + has_before + groups * (takes_lower + takes_upper)
    pl.semaphore_wait(barrier, count + groups - 2 + rims)

    row_scale = row_scale_ref[...]
    stiffness = stiffness_ref[...]
    base = base_ref[...]
    friction = friction_ref[...]
    damping = damping_ref[...]
    inverse_friction = 1.0 / friction

    def target(shift):
        if count & (count - 1):
            return lax.rem(patch + shift, count)
        place = patch
        bit = 1
        while bit < count:
            if shift & bit:
                place = place + bit - 2 * bit * lax.rem(lax.div(patch, bit), 2)
            bit *= 2
        return place

    def source(shift):
        if count & (count - 1):
            return lax.rem(patch + count - shift, count)
        return target(shift)

    stage = [0]

    def stress_of(deficit):
        slot = stage[0] % 2
        mine = gathered.at[slot, patch, 0:members]
        gathered[slot, patch] = deficit.astype(jnp.bfloat16)
        copies = []
        for shift in reversed(range(1, count)):
            copy = pltpu.make_async_remote_copy(
                src_ref=mine,
                dst_ref=mine,
                send_sem=gather_send.at[slot, shift],
                recv_sem=gather_recv.at[slot, shift],
                device_id=(member, target(shift)),
                device_id_type=MESH,
            )
            copy.start()
            copies.append(copy)
        if stage[0] == 0:
            load.wait()
        summed = jnp.zeros((rows, own), jnp.float32)
        for shift in range(count):
            origin = source(shift)
            if shift:
                theirs = gathered.at[slot, origin, 0:members]
                pltpu.make_async_remote_copy(
                    src_ref=theirs,
                    dst_ref=theirs,
                    send_sem=gather_send.at[slot, shift],
                    recv_sem=gather_recv.at[slot, shift],
                    device_id=(member, origin),
                    device_id_type=MESH,
                ).wait_recv()
            columns = pl.ds(pl.multiple_of(origin * own, LANES), own)
            summed = summed + lax.dot_general(
                gathered[slot, origin],
                kernel_ref[:, columns],
                (((1,), (1,)), ((), ())),
                preferred_element_type=jnp.float32,
            )
        for copy in copies:
            copy.wait_send()
        stage[0] += 1
        return base + stiffness * deficit + row_scale * summed

    def rate(deficit, state_log, guess):
        return slip_rate(
            stress_of(deficit), state_log, guess, friction, inverse_friction, damping
        )

    def tendency(deficit, state_log, guess):
        velocity = rate(deficit, state_log, guess)
        return (plate_rate - velocity, jnp.exp(-state_log) - jnp.abs(velocity), velocity)

    deficit = start_ref[0]
    state_log = start_ref[1]
    velocity = jnp.zeros_like(deficit)
    for _ in range(STEPS):
        deficit_zero, state_zero = (deficit, state_log)
        change, state_change, velocity = tendency(deficit_zero, state_zero, velocity)
        deficit_one = deficit_zero + time_step * change
        state_one = state_zero + time_step * state_change
        change, state_change, velocity = tendency(deficit_one, state_one, velocity)
        deficit_two = 0.75 * deficit_zero + 0.25 * (deficit_one + time_step * change)
        state_two = 0.75 * state_zero + 0.25 * (state_one + time_step * state_change)
        change, state_change, velocity = tendency(deficit_two, state_two, velocity)
        deficit = deficit_zero / 3.0 + 2.0 / 3.0 * (deficit_two + time_step * change)
        state_log = state_zero / 3.0 + 2.0 / 3.0 * (state_two + time_step * state_change)
    velocity = rate(deficit, state_log, velocity)

    row = lax.broadcasted_iota(jnp.int32, (rows, own), 0)
    joined = jnp.where(row == members, obs_rate_ref[...], velocity)
    joined = jnp.where(row == members + 1, obs_precision_ref[...], joined)

    def window(cells, first):
        return pltpu.roll(cells, (-first) % own, 1)[:, :LANES]

    for group in range(groups):
        packed[group, 0:rows] = window(joined, group * sub_block - MARGIN)
        packed[group, rows : 2 * rows] = window(deficit, group * sub_block)
        packed[group, 2 * rows :] = window(state_log, group * sub_block)

    def move(shift):
        other = lax.rem(member + shift, groups)
        return pltpu.make_async_remote_copy(
            src_ref=packed.at[other],
            dst_ref=landed.at[shift],
            send_sem=move_send.at[shift],
            recv_sem=move_recv.at[shift],
            device_id=(other, patch),
            device_id_type=MESH,
        )

    def right_rim():
        return pltpu.make_async_remote_copy(
            src_ref=packed.at[0, 0:rows],
            dst_ref=lower.at[member],
            send_sem=rim_send.at[0],
            recv_sem=rim_recv.at[0, member],
            device_id=(0, after),
            device_id_type=MESH,
        )

    def left_rim():
        return pltpu.make_async_remote_copy(
            src_ref=packed.at[last, 0:rows],
            dst_ref=upper.at[member],
            send_sem=rim_send.at[1],
            recv_sem=rim_recv.at[1, member],
            device_id=(last, before),
            device_id_type=MESH,
        )

    @pl.when(has_after > 0)
    def _():
        right_rim().start()

    @pl.when(has_before > 0)
    def _():
        left_rim().start()

    for shift in range(1, groups):
        move(shift).start()

    landed[0] = packed[member]

    @pl.when(takes_lower > 0)
    def _():
        for other in range(groups):
            pltpu.make_async_remote_copy(
                src_ref=packed.at[0, 0:rows],
                dst_ref=lower.at[other],
                send_sem=rim_send.at[0],
                recv_sem=rim_recv.at[0, other],
                device_id=(other, before),
                device_id_type=MESH,
            ).wait_recv()

    @pl.when(takes_upper > 0)
    def _():
        for other in range(groups):
            pltpu.make_async_remote_copy(
                src_ref=packed.at[0, 0:rows],
                dst_ref=upper.at[other],
                send_sem=rim_send.at[1],
                recv_sem=rim_recv.at[1, other],
                device_id=(other, after),
                device_id_type=MESH,
            ).wait_recv()

    for shift in range(1, groups):
        move(shift).wait_recv()

    lane = lax.broadcasted_iota(jnp.int32, (rows, LANES), 1)
    below = jnp.logical_and(lane < MARGIN, member == 0)
    above = jnp.logical_and(lane >= MARGIN + sub_block, member == last)
    start = jnp.logical_and(below, patch == 0)
    end = jnp.logical_and(above, patch == count - 1)
    outside = jnp.logical_or(start, jnp.logical_or(end, lane >= sub_block + 2 * MARGIN))
    for other in range(groups):
        held = landed[lax.rem(member - other + groups, groups)]
        cells = jnp.where(below, lower[other], held[0:rows])
        cells = jnp.where(above, upper[other], cells)
        cells = jnp.where(outside, 0.0, cells)
        fields_out[other, 0] = cells
        fields_out[other, 1] = held[rows : 2 * rows]
        fields_out[other, 2] = held[2 * rows :]

    for shift in range(1, groups):
        move(shift).wait_send()

    @pl.when(has_after > 0)
    def _():
        right_rim().wait_send()

    @pl.when(has_before > 0)
    def _():
        left_rim().wait_send()


def analysis_kernel(members, sub_block, fields_ref, out_ref, cross, mixing, kept, halfway):
    groups = fields_ref.shape[0]
    ensemble = groups * members
    split = LANES // sub_block
    per = ensemble // split
    extra = kept.shape[0] - per
    step = 24

    lane_row = lax.broadcasted_iota(jnp.int32, (1, LANES), 1)
    part = lane_row // sub_block

    def stacked(which):
        return jnp.concatenate(
            [fields_ref[g, which, 0:members] for g in range(groups)], axis=0
        )

    rates = stacked(0)
    observed = fields_ref[0, 0, members : members + 2]
    mean_rate = jnp.sum(rates, axis=0, keepdims=True) / ensemble
    anomalies = rates - mean_rate
    innovation = observed[0:1] - mean_rate
    weighted = anomalies * observed[1:2]

    source = lax.broadcasted_iota(jnp.int32, (LANES, LANES), 0)
    target = lax.broadcasted_iota(jnp.int32, (LANES, LANES), 1) % sub_block
    distance = jnp.abs(target + MARGIN - source).astype(jnp.float32)
    tapering = jnp.where(distance <= MARGIN, jnp.exp(-0.5 * (distance / MARGIN) ** 2), 0.0)

    def smooth(cells):
        return lax.dot_general(
            cells,
            tapering,
            (((1,), (0,)), ((), ())),
            precision=lax.Precision.HIGHEST,
            preferred_element_type=jnp.float32,
        )

    drive = smooth(weighted * innovation)
    trace = jnp.zeros((1, LANES), jnp.float32)
    for first in range(0, ensemble, step):
        products = jnp.concatenate(
            [weighted * anomalies[m : m + 1] for m in range(first, first + step)], axis=0
        )
        smoothed = smooth(products).reshape(step, ensemble, LANES)
        cross[first : first + step] = smoothed
        for m in range(step):
            trace = trace + smoothed[m, first + m : first + m + 1]
    scaling = ensemble - 1.0 + trace
    inverse_scaling = 1.0 / scaling

    column = lax.broadcasted_iota(jnp.int32, (ensemble, LANES), 0)

    def unit(m):
        return jnp.where(column == m, 1.0, 0.0)

    for m in range(ensemble):
        root = ((ensemble - 1.0) * unit(m) + cross[m]) * inverse_scaling
        mixing[m] = 1.5 * unit(m) - 0.5 * root
        cross[m] = root
    for r in range(per):
        root = cross[r]
        for g in range(1, split):
            root = jnp.where(part == g, cross[g * per + r], root)
        kept[r] = root

    fields = [stacked(1), stacked(2), pltpu.roll(rates, LANES - MARGIN, 1)]
    means = [jnp.sum(field, axis=0, keepdims=True) / ensemble for field in fields]
    vectors = [field - mean for field, mean in zip(fields, means)]
    for e in range(extra):
        filled = jnp.zeros((ensemble, LANES), jnp.float32)
        for t in range(e * split, min(e * split + split, 4)):
            g = t % split
            if t == 3:
                cells = drive
            else:
                cells = vectors[t]
                if g:
                    cells = pltpu.roll(cells, g * sub_block, 1)
            filled = jnp.where(part == g, cells, filled)
        kept[per + e] = filled

    def product(left, lo, hi, store):
        for first in range(0, ensemble, step):

            def some(base, sums):
                for k in range(TILE):
                    row = mixing[base + k, first : first + step]
                    sums = [
                        total + left[lo + i, pl.ds(base + k, 1)] * row
                        for i, total in enumerate(sums)
                    ]
                return sums

            sums = [jnp.zeros((step, LANES), jnp.float32) for _ in range(hi - lo)]
            if ensemble <= step:
                for base in range(0, ensemble, TILE):
                    sums = some(base, sums)
            else:
                sums = lax.fori_loop(
                    0, ensemble // TILE, lambda b, s: some(b * TILE, s), sums
                )
            for i, total in enumerate(sums):
                store(lo + i, first, total)

    def into(target):
        def store(i, first, total):
            target[i, first : first + step] = total

        return store

    def remix():
        for r in range(per):
            cells = kept[r]
            if split == 2:
                other = pltpu.roll(cells, sub_block, 1)
                spread = [jnp.where(part == 0, cells, other), jnp.where(part == 0, other, cells)]
            else:
                spread = []
                for g in range(split):
                    one = jnp.where(part == g, cells, 0.0)
                    width = sub_block
                    while width < LANES:
                        one = one + pltpu.roll(one, width, 1)
                        width *= 2
                    spread.append(one)
            for g in range(split):
                m = g * per + r
                mixing[m] = 1.5 * unit(m) - 0.5 * spread[g]

    def iterate(_, carry):
        product(kept, 0, per + extra, into(halfway))
        for e in range(extra):
            kept[per + e] = halfway[per + e]
        product(halfway, 0, per, into(kept))
        remix()
        return carry

    lax.fori_loop(0, NS_ITERS - 1, iterate, 0)
    product(kept, per, per + extra, into(halfway))

    def taken(t):
        cells = halfway[per + t // split]
        g = t % split
        return pltpu.roll(cells, LANES - g * sub_block, 1) if g else cells

    driven = taken(3)
    widening = math.sqrt(ensemble - 1.0) * lax.rsqrt(scaling)
    for v in range(3):
        spread = taken(v)
        moved = jnp.sum(spread * driven, axis=0, keepdims=True) * inverse_scaling
        result = means[v] + moved + widening * spread
        out_ref[v] = result[:, :sub_block]


def body(
    groups,
    count,
    kernel_rows,
    row_scale,
    self_stiffness,
    base_stress,
    friction_rate,
    damping,
    deficit_start,
    state_start,
    obs_rate,
    obs_precision,
):
    own, patches = kernel_rows.shape
    members = deficit_start.shape[0]
    ensemble = members * groups
    sub_block = own // groups
    rows = -(-(members + 2) // TILE) * TILE
    vmem = pl.BlockSpec(memory_space=pltpu.VMEM)
    f32 = jnp.float32

    fields = pl.pallas_call(
        functools.partial(forecast_kernel, groups, count),
        out_shape=jax.ShapeDtypeStruct((groups, 3, rows, LANES), f32),
        in_specs=[pl.BlockSpec(memory_space=pl.ANY)] + [vmem] * 9,
        out_specs=vmem,
        scratch_shapes=[
            pltpu.VMEM((own, patches), jnp.bfloat16),
            pltpu.VMEM((2, rows, own), f32),
            pltpu.VMEM((2, count, rows, own), jnp.bfloat16),
            pltpu.VMEM((groups, 3 * rows, LANES), f32),
            pltpu.VMEM((groups, 3 * rows, LANES), f32),
            pltpu.VMEM((groups, rows, LANES), f32),
            pltpu.VMEM((groups, rows, LANES), f32),
            pltpu.SemaphoreType.DMA,
            pltpu.SemaphoreType.DMA((2, count)),
            pltpu.SemaphoreType.DMA((2, count)),
            pltpu.SemaphoreType.DMA((groups,)),
            pltpu.SemaphoreType.DMA((groups,)),
            pltpu.SemaphoreType.DMA((2,)),
            pltpu.SemaphoreType.DMA((2, groups)),
        ],
        compiler_params=pltpu.CompilerParams(collective_id=0, has_side_effects=True),
    )(
        kernel_rows,
        *(
            cells.reshape(1, own)
            for cells in (row_scale, self_stiffness, base_stress, friction_rate, damping)
        ),
        deficit_start,
        state_start,
        obs_rate.reshape(1, own),
        obs_precision.reshape(1, own),
    )

    split = LANES // sub_block
    per = ensemble // split
    extra = -(-4 // split)
    analysis = pl.pallas_call(
        functools.partial(analysis_kernel, members, sub_block),
        out_shape=jax.ShapeDtypeStruct((3, ensemble, sub_block), f32),
        in_specs=[vmem],
        out_specs=vmem,
        scratch_shapes=[
            pltpu.VMEM((ensemble, ensemble, LANES), f32),
            pltpu.VMEM((ensemble, ensemble, LANES), f32),
            pltpu.VMEM((per + extra, ensemble, LANES), f32),
            pltpu.VMEM((per + extra, ensemble, LANES), f32),
        ],
    )(fields)
    return analysis[:, :, None, :]


def solution(mesh):
    return jax.shard_map(
        functools.partial(body, mesh.shape["member"], mesh.shape["patch"]),
        mesh=mesh,
        in_specs=(
            P("patch", None),
            P("patch"),
            P("patch"),
            P("patch"),
            P("patch"),
            P("patch"),
            P("member", "patch"),
            P("member", "patch"),
            P("patch"),
            P("patch"),
        ),
        out_specs=P(None, None, "patch", "member"),
        check_vma=False,
    )
```

```python
import functools
import math

import jax
import jax.numpy as jnp
from jax import lax
from jax.experimental import pallas as pl
from jax.experimental.pallas import tpu as pltpu
from jax.sharding import PartitionSpec as P

STEPS = 2
NEWTON = 4
NS_ITERS = 6
MARGIN = 8
LANES = 128
TILE = 8

time_step = 0.25
plate_rate = 1.0

MESH = pl.DeviceIdType.MESH


def slip_rate(stress, state_log, guess, friction, inverse_friction, damping):
    factor = 0.5 * jnp.exp(state_log * inverse_friction)
    slope = friction * factor
    velocity = guess
    for _ in range(NEWTON):
        scaled = factor * velocity
        square = 1.0 + scaled * scaled
        inverse = lax.rsqrt(square)
        grown = jnp.log(jnp.abs(scaled) + square * inverse)
        grown = jnp.where(scaled < 0, -grown, grown)
        residual = friction * grown + damping * velocity - stress
        velocity = velocity - residual / (slope * inverse + damping)
    return velocity


def forecast_kernel(
    groups,
    count,
    kernel_hbm,
    *rest,
):
    sources, fields_out, held_here, rest = rest[:9], rest[9], rest[10:19], rest[19:]
    kernel_ref, start_ref, gathered, packed, landed, lower, upper, small_sem, *rest = rest
    load_sem, gather_send, gather_recv, move_send, move_recv, rim_send, rim_recv = rest
    row_scale_ref, stiffness_ref, base_ref, friction_ref, damping_ref = held_here[:5]
    deficit_ref, state_ref, obs_rate_ref, obs_precision_ref = held_here[5:]
    member = lax.axis_index("member")
    patch = lax.axis_index("patch")
    members, own = deficit_ref.shape
    rows = start_ref.shape[1]
    sub_block = own // groups
    last = groups - 1

    small = [
        pltpu.make_async_copy(source, here, small_sem.at[i])
        for i, (source, here) in enumerate(zip(sources, held_here))
    ]
    for copy in small:
        copy.start()
    load = pltpu.make_async_copy(kernel_hbm, kernel_ref, load_sem)
    load.start()

    gathered[...] = jnp.zeros_like(gathered)
    lower[...] = jnp.zeros_like(lower)
    upper[...] = jnp.zeros_like(upper)
    start_ref[...] = jnp.zeros_like(start_ref)

    barrier = pltpu.get_barrier_semaphore()

    def greet(where):
        pl.semaphore_signal(barrier, inc=1, device_id=where, device_id_type=MESH)

    for shift in range(1, count):
        greet((member, lax.rem(patch + shift, count)))
    for shift in range(1, groups):
        greet((lax.rem(member + shift, groups), patch))

    after = lax.rem(patch + 1, count)
    before = lax.rem(patch + count - 1, count)
    has_after = 1 - lax.div(patch + 1, count)
    has_before = lax.div(patch + count - 1, count)
    takes_lower = (1 - lax.div(member + last, groups)) * has_before
    takes_upper = lax.div(member + 1, groups) * has_after

    @pl.when(has_after > 0)
    def _():
        greet((0, after))

    @pl.when(has_before > 0)
    def _():
        greet((last, before))

    @pl.when(takes_lower > 0)
    def _():
        for other in range(groups):
            greet((other, before))

    @pl.when(takes_upper > 0)
    def _():
        for other in range(groups):
            greet((other, after))

    for copy in small:
        copy.wait()
    start_ref[0, 0:members] = deficit_ref[...]
    start_ref[1, 0:members] = state_ref[...]

    rims = has_after + has_before + groups * (takes_lower + takes_upper)
    pl.semaphore_wait(barrier, count + groups - 2 + rims)

    row_scale = row_scale_ref[...]
    stiffness = stiffness_ref[...]
    base = base_ref[...]
    friction = friction_ref[...]
    damping = damping_ref[...]
    inverse_friction = 1.0 / friction

    def target(shift):
        if count & (count - 1):
            return lax.rem(patch + shift, count)
        place = patch
        bit = 1
        while bit < count:
            if shift & bit:
                place = place + bit - 2 * bit * lax.rem(lax.div(patch, bit), 2)
            bit *= 2
        return place

    def source(shift):
        if count & (count - 1):
            return lax.rem(patch + count - shift, count)
        return target(shift)

    stage = [0]
    pending = []

    def stress_of(deficit, meanwhile=None):
        slot = stage[0] % 2
        mine = gathered.at[slot, patch, 0:members]
        gathered[slot, patch] = deficit.astype(jnp.bfloat16)
        copies = []
        for shift in reversed(range(1, count)):
            copy = pltpu.make_async_remote_copy(
                src_ref=mine,
                dst_ref=mine,
                send_sem=gather_send.at[slot, shift],
                recv_sem=gather_recv.at[slot, shift],
                device_id=(member, target(shift)),
                device_id_type=MESH,
            )
            copy.start()
            copies.append(copy)
        pending.append(copies)
        if meanwhile is not None:
            meanwhile()
        if stage[0] == 0:
            load.wait()
        summed = jnp.zeros((rows, own), jnp.float32)
        for shift in range(count):
            origin = source(shift)
            if shift:
                theirs = gathered.at[slot, origin, 0:members]
                pltpu.make_async_remote_copy(
                    src_ref=theirs,
                    dst_ref=theirs,
                    send_sem=gather_send.at[slot, shift],
                    recv_sem=gather_recv.at[slot, shift],
                    device_id=(member, origin),
                    device_id_type=MESH,
                ).wait_recv()
            columns = pl.ds(pl.multiple_of(origin * own, LANES), own)
            summed = summed + lax.dot_general(
                gathered[slot, origin],
                kernel_ref[:, columns],
                (((1,), (1,)), ((), ())),
                preferred_element_type=jnp.float32,
            )
        while len(pending) > 1 or (pending and stage[0] == 3 * STEPS):
            for copy in pending.pop(0):
                copy.wait_send()
        stage[0] += 1
        return base + stiffness * deficit + row_scale * summed

    def rate(deficit, state_log, guess, meanwhile=None):
        stress = stress_of(deficit, meanwhile)
        return slip_rate(stress, state_log, guess, friction, inverse_friction, damping)

    def tendency(deficit, state_log, guess):
        velocity = rate(deficit, state_log, guess)
        return (plate_rate - velocity, jnp.exp(-state_log) - jnp.abs(velocity), velocity)

    deficit = start_ref[0]
    state_log = start_ref[1]
    velocity = jnp.zeros_like(deficit)
    for _ in range(STEPS):
        deficit_zero, state_zero = (deficit, state_log)
        change, state_change, velocity = tendency(deficit_zero, state_zero, velocity)
        deficit_one = deficit_zero + time_step * change
        state_one = state_zero + time_step * state_change
        change, state_change, velocity = tendency(deficit_one, state_one, velocity)
        deficit_two = 0.75 * deficit_zero + 0.25 * (deficit_one + time_step * change)
        state_two = 0.75 * state_zero + 0.25 * (state_one + time_step * state_change)
        change, state_change, velocity = tendency(deficit_two, state_two, velocity)
        deficit = deficit_zero / 3.0 + 2.0 / 3.0 * (deficit_two + time_step * change)
        state_log = state_zero / 3.0 + 2.0 / 3.0 * (state_two + time_step * state_change)
    def window(cells, first):
        return pltpu.roll(cells, (-first) % own, 1)[:, :LANES]

    def move(which, shift):
        lo, size = (0, rows) if which == 0 else (rows, 2 * rows)
        other = lax.rem(member + shift, groups)
        return pltpu.make_async_remote_copy(
            src_ref=packed.at[other, lo : lo + size],
            dst_ref=landed.at[shift, lo : lo + size],
            send_sem=move_send.at[which, shift],
            recv_sem=move_recv.at[which, shift],
            device_id=(other, patch),
            device_id_type=MESH,
        )

    def send_states():
        for group in range(groups):
            packed[group, rows : 2 * rows] = window(deficit, group * sub_block)
            packed[group, 2 * rows :] = window(state_log, group * sub_block)
        for shift in range(1, groups):
            move(1, shift).start()

    velocity = rate(deficit, state_log, velocity, send_states)

    row = lax.broadcasted_iota(jnp.int32, (rows, own), 0)
    joined = jnp.where(row == members, obs_rate_ref[...], velocity)
    joined = jnp.where(row == members + 1, obs_precision_ref[...], joined)
    for group in range(groups):
        packed[group, 0:rows] = window(joined, group * sub_block - MARGIN)

    def right_rim():
        return pltpu.make_async_remote_copy(
            src_ref=packed.at[0, 0:rows],
            dst_ref=lower.at[member],
            send_sem=rim_send.at[0],
            recv_sem=rim_recv.at[0, member],
            device_id=(0, after),
            device_id_type=MESH,
        )

    def left_rim():
        return pltpu.make_async_remote_copy(
            src_ref=packed.at[last, 0:rows],
            dst_ref=upper.at[member],
            send_sem=rim_send.at[1],
            recv_sem=rim_recv.at[1, member],
            device_id=(last, before),
            device_id_type=MESH,
        )

    @pl.when(has_after > 0)
    def _():
        right_rim().start()

    @pl.when(has_before > 0)
    def _():
        left_rim().start()

    for shift in range(1, groups):
        move(0, shift).start()

    landed[0] = packed[member]

    @pl.when(takes_lower > 0)
    def _():
        for other in range(groups):
            pltpu.make_async_remote_copy(
                src_ref=packed.at[0, 0:rows],
                dst_ref=lower.at[other],
                send_sem=rim_send.at[0],
                recv_sem=rim_recv.at[0, other],
                device_id=(other, before),
                device_id_type=MESH,
            ).wait_recv()

    @pl.when(takes_upper > 0)
    def _():
        for other in range(groups):
            pltpu.make_async_remote_copy(
                src_ref=packed.at[0, 0:rows],
                dst_ref=upper.at[other],
                send_sem=rim_send.at[1],
                recv_sem=rim_recv.at[1, other],
                device_id=(other, after),
                device_id_type=MESH,
            ).wait_recv()

    for shift in range(1, groups):
        move(1, shift).wait_recv()
        move(0, shift).wait_recv()

    lane = lax.broadcasted_iota(jnp.int32, (rows, LANES), 1)
    below = jnp.logical_and(lane < MARGIN, member == 0)
    above = jnp.logical_and(lane >= MARGIN + sub_block, member == last)
    start = jnp.logical_and(below, patch == 0)
    end = jnp.logical_and(above, patch == count - 1)
    outside = jnp.logical_or(start, jnp.logical_or(end, lane >= sub_block + 2 * MARGIN))
    for other in range(groups):
        held = landed[lax.rem(member - other + groups, groups)]
        cells = jnp.where(below, lower[other], held[0:rows])
        cells = jnp.where(above, upper[other], cells)
        cells = jnp.where(outside, 0.0, cells)
        fields_out[other, 0] = cells
        fields_out[other, 1] = held[rows : 2 * rows]
        fields_out[other, 2] = held[2 * rows :]

    for shift in range(1, groups):
        move(1, shift).wait_send()
        move(0, shift).wait_send()

    @pl.when(has_after > 0)
    def _():
        right_rim().wait_send()

    @pl.when(has_before > 0)
    def _():
        left_rim().wait_send()


def analysis_kernel(members, sub_block, fields_ref, out_ref, cross, mixing, kept, halfway):
    groups = fields_ref.shape[0]
    ensemble = groups * members
    split = LANES // sub_block
    per = ensemble // split
    extra = kept.shape[0] - per
    step = 24

    lane_row = lax.broadcasted_iota(jnp.int32, (1, LANES), 1)
    part = lane_row // sub_block

    def stacked(which):
        return jnp.concatenate(
            [fields_ref[g, which, 0:members] for g in range(groups)], axis=0
        )

    rates = stacked(0)
    observed = fields_ref[0, 0, members : members + 2]
    mean_rate = jnp.sum(rates, axis=0, keepdims=True) / ensemble
    anomalies = rates - mean_rate
    innovation = observed[0:1] - mean_rate
    weighted = anomalies * observed[1:2]

    source = lax.broadcasted_iota(jnp.int32, (LANES, LANES), 0)
    target = lax.broadcasted_iota(jnp.int32, (LANES, LANES), 1) % sub_block
    distance = jnp.abs(target + MARGIN - source).astype(jnp.float32)
    tapering = jnp.where(distance <= MARGIN, jnp.exp(-0.5 * (distance / MARGIN) ** 2), 0.0)

    def smooth(cells):
        return lax.dot_general(
            cells,
            tapering,
            (((1,), (0,)), ((), ())),
            precision=lax.Precision.HIGHEST,
            preferred_element_type=jnp.float32,
        )

    drive = smooth(weighted * innovation)
    trace = jnp.zeros((1, LANES), jnp.float32)
    for first in range(0, ensemble, step):
        products = jnp.concatenate(
            [weighted * anomalies[m : m + 1] for m in range(first, first + step)], axis=0
        )
        smoothed = smooth(products).reshape(step, ensemble, LANES)
        cross[first : first + step] = smoothed
        for m in range(step):
            trace = trace + smoothed[m, first + m : first + m + 1]
    scaling = ensemble - 1.0 + trace
    inverse_scaling = 1.0 / scaling

    column = lax.broadcasted_iota(jnp.int32, (ensemble, LANES), 0)

    def unit(m):
        return jnp.where(column == m, 1.0, 0.0)

    for m in range(ensemble):
        root = ((ensemble - 1.0) * unit(m) + cross[m]) * inverse_scaling
        mixing[m] = 1.5 * unit(m) - 0.5 * root
        cross[m] = root
    for r in range(per):
        root = cross[r]
        for g in range(1, split):
            root = jnp.where(part == g, cross[g * per + r], root)
        kept[r] = root

    fields = [stacked(1), stacked(2), pltpu.roll(rates, LANES - MARGIN, 1)]
    means = [jnp.sum(field, axis=0, keepdims=True) / ensemble for field in fields]
    vectors = [field - mean for field, mean in zip(fields, means)]
    for e in range(extra):
        filled = jnp.zeros((ensemble, LANES), jnp.float32)
        for t in range(e * split, min(e * split + split, 4)):
            g = t % split
            if t == 3:
                cells = drive
            else:
                cells = vectors[t]
                if g:
                    cells = pltpu.roll(cells, g * sub_block, 1)
            filled = jnp.where(part == g, cells, filled)
        kept[per + e] = filled

    def product(left, lo, hi, store):
        for first in range(0, ensemble, step):

            def some(base, sums):
                for k in range(TILE):
                    row = mixing[base + k, first : first + step]
                    sums = [
                        total + left[lo + i, pl.ds(base + k, 1)] * row
                        for i, total in enumerate(sums)
                    ]
                return sums

            sums = [jnp.zeros((step, LANES), jnp.float32) for _ in range(hi - lo)]
            if ensemble <= step:
                for base in range(0, ensemble, TILE):
                    sums = some(base, sums)
            else:
                sums = lax.fori_loop(
                    0, ensemble // TILE, lambda b, s: some(b * TILE, s), sums
                )
            for i, total in enumerate(sums):
                store(lo + i, first, total)

    def into(target):
        def store(i, first, total):
            target[i, first : first + step] = total

        return store

    def remix():
        for r in range(per):
            cells = kept[r]
            if split == 2:
                other = pltpu.roll(cells, sub_block, 1)
                spread = [jnp.where(part == 0, cells, other), jnp.where(part == 0, other, cells)]
            else:
                spread = []
                for g in range(split):
                    one = jnp.where(part == g, cells, 0.0)
                    width = sub_block
                    while width < LANES:
                        one = one + pltpu.roll(one, width, 1)
                        width *= 2
                    spread.append(one)
            for g in range(split):
                m = g * per + r
                mixing[m] = 1.5 * unit(m) - 0.5 * spread[g]

    def iterate(_, carry):
        product(kept, 0, per + extra, into(halfway))
        for e in range(extra):
            kept[per + e] = halfway[per + e]
        product(halfway, 0, per, into(kept))
        remix()
        return carry

    lax.fori_loop(0, NS_ITERS - 1, iterate, 0)
    product(kept, per, per + extra, into(halfway))

    def taken(t):
        cells = halfway[per + t // split]
        g = t % split
        return pltpu.roll(cells, LANES - g * sub_block, 1) if g else cells

    driven = taken(3)
    widening = math.sqrt(ensemble - 1.0) * lax.rsqrt(scaling)
    for v in range(3):
        spread = taken(v)
        moved = jnp.sum(spread * driven, axis=0, keepdims=True) * inverse_scaling
        result = means[v] + moved + widening * spread
        out_ref[v] = result[:, :sub_block]


def body(
    groups,
    count,
    kernel_rows,
    row_scale,
    self_stiffness,
    base_stress,
    friction_rate,
    damping,
    deficit_start,
    state_start,
    obs_rate,
    obs_precision,
):
    own, patches = kernel_rows.shape
    members = deficit_start.shape[0]
    ensemble = members * groups
    sub_block = own // groups
    rows = -(-(members + 2) // TILE) * TILE
    vmem = pl.BlockSpec(memory_space=pltpu.VMEM)
    f32 = jnp.float32

    fields = pl.pallas_call(
        functools.partial(forecast_kernel, groups, count),
        out_shape=jax.ShapeDtypeStruct((groups, 3, rows, LANES), f32),
        in_specs=[pl.BlockSpec(memory_space=pl.ANY)] * 10,
        out_specs=vmem,
        scratch_shapes=[pltpu.VMEM((1, own), f32)] * 5
        + [pltpu.VMEM((members, own), f32)] * 2
        + [pltpu.VMEM((1, own), f32)] * 2
        + [
            pltpu.VMEM((own, patches), jnp.bfloat16),
            pltpu.VMEM((2, rows, own), f32),
            pltpu.VMEM((2, count, rows, own), jnp.bfloat16),
            pltpu.VMEM((groups, 3 * rows, LANES), f32),
            pltpu.VMEM((groups, 3 * rows, LANES), f32),
            pltpu.VMEM((groups, rows, LANES), f32),
            pltpu.VMEM((groups, rows, LANES), f32),
            pltpu.SemaphoreType.DMA((9,)),
            pltpu.SemaphoreType.DMA,
            pltpu.SemaphoreType.DMA((2, count)),
            pltpu.SemaphoreType.DMA((2, count)),
            pltpu.SemaphoreType.DMA((2, groups)),
            pltpu.SemaphoreType.DMA((2, groups)),
            pltpu.SemaphoreType.DMA((2,)),
            pltpu.SemaphoreType.DMA((2, groups)),
        ],
        compiler_params=pltpu.CompilerParams(collective_id=0, has_side_effects=True),
    )(
        kernel_rows,
        *(
            cells.reshape(1, own)
            for cells in (row_scale, self_stiffness, base_stress, friction_rate, damping)
        ),
        deficit_start,
        state_start,
        obs_rate.reshape(1, own),
        obs_precision.reshape(1, own),
    )

    split = LANES // sub_block
    per = ensemble // split
    extra = -(-4 // split)
    analysis = pl.pallas_call(
        functools.partial(analysis_kernel, members, sub_block),
        out_shape=jax.ShapeDtypeStruct((3, ensemble, sub_block), f32),
        in_specs=[vmem],
        out_specs=vmem,
        scratch_shapes=[
            pltpu.VMEM((ensemble, ensemble, LANES), f32),
            pltpu.VMEM((ensemble, ensemble, LANES), f32),
            pltpu.VMEM((per + extra, ensemble, LANES), f32),
            pltpu.VMEM((per + extra, ensemble, LANES), f32),
        ],
    )(fields)
    return analysis[:, :, None, :]


def solution(mesh):
    return jax.shard_map(
        functools.partial(body, mesh.shape["member"], mesh.shape["patch"]),
        mesh=mesh,
        in_specs=(
            P("patch", None),
            P("patch"),
            P("patch"),
            P("patch"),
            P("patch"),
            P("patch"),
            P("member", "patch"),
            P("member", "patch"),
            P("patch"),
            P("patch"),
        ),
        out_specs=P(None, None, "patch", "member"),
        check_vma=False,
    )
```
